1024 devices in a mesh: gz: 64 (over y_hi, z), gy: 16 (over x, y_lo, core).
Axes of the slice: x: 4, y: 4 (y_hi: 2, y_lo: 2; y = y_hi * 2 + y_lo), z: 32, core: 2. Of those that a mesh axis runs over, the one named last changes fastest.
Arguments:
- state: bfloat16 [5, 8, 768, 1536], P(None, None, 'gy', 'gz'), may hold values from -6 to 6
- visc_base: bfloat16 [8, 768, 1536], P(None, 'gy', 'gz'), may hold values from 0.29882812 to 3
- dz_op: bfloat16 [1536, 1536], replicated, may hold values from -0.15625 to 0.15625
- dy_op: bfloat16 [768, 768], replicated, may hold values from -0.21875 to 0.21875
Outputs:
- new_state: bfloat16 [5, 8, 768, 1536], P(None, None, 'gy', 'gz')
The draws below stay inside these ranges and needn't reach their ends.
All inputs are finite; a program needn't handle non-finite values.
Results may differ from the reference program's by a relative error of at most 0.011.
Values may be sent and summed in bfloat16 or wider, within the bound.
No kernel may reach another device: no remote copies, remote signals or barrier semaphores. Data moves between devices by JAX's collectives and lax.ppermute only.
A program may use at most 32 MiB of HBM per device.

```python
import math
import jax
import jax.numpy as jnp
from jax import lax

FIELDS = 5
X = 8
NY = 768
NZ = 1536


def levels(own_key, shape, cuts, smallest, high):
    gain, own = 1.0, jax.random.fold_in(own_key, 6)
    for dim, shards_of in cuts:
        heights = jnp.exp(jax.random.uniform(jax.random.fold_in(own, dim), (shards_of,), jnp.float32, smallest / len(cuts), high / len(cuts)))
        gain = gain * jnp.repeat(heights, shape[dim] // shards_of).reshape([-1 if axis == dim else 1 for axis in range(len(shape))])
    return gain


def bell_draw(own_key, dims, deviation, reach, pieces=(), held_as=jnp.bfloat16):
    values = jax.random.normal(own_key, dims, jnp.float32) * deviation
    if len(pieces) > 0:
        values = levels(own_key, dims, pieces, -0.22, 0.18) * values
    return jnp.clip(values, min=-reach, max=reach).astype(held_as)


def setup_inputs(seed: int = 0) -> dict:
    streams_of = jax.random.split(jax.random.key(seed), 5)
    return {
        "state": bell_draw(streams_of[0], (FIELDS, X, NY, NZ), 1.0, 6.0, ((2, 16), (3, 64))),
        "visc_base": jnp.clip(jnp.exp(math.log(3.0) - 2.306499 * jax.random.uniform(streams_of[1], (X, NY, NZ), jnp.float32) ** levels(streams_of[1], (X, NY, NZ), ((1, 16), (2, 64)), -0.2, 0.2)), 0.29882812, 3.0).astype(jnp.bfloat16),
        "dz_op": bell_draw(streams_of[2], (NZ, NZ), NZ ** -0.5, 0.15625),
        "dy_op": bell_draw(streams_of[3], (NY, NY), NY ** -0.5, 0.21875),
    }


def zline_apply(field, operator):
    result = jnp.dot(field.reshape(-1, operator.shape[0]), operator, preferred_element_type=jnp.float32)
    return result.astype(jnp.bfloat16).reshape(field.shape)


def yline_apply(field, operator):
    turned = jnp.swapaxes(field, 1, 2)
    result = jnp.dot(turned.reshape(-1, operator.shape[0]), operator, preferred_element_type=jnp.float32)
    return jnp.swapaxes(result.astype(jnp.bfloat16).reshape(turned.shape), 1, 2)


def reference(state, visc_base, dz_op, dy_op):
    grad_z = lax.map(lambda field: zline_apply(field, dz_op), state)
    grad_y = lax.map(lambda field: yline_apply(field, dy_op), state)
    sensor = grad_y[0].astype(jnp.float32) ** 2 + grad_z[0].astype(jnp.float32) ** 2
    visc = (visc_base.astype(jnp.float32) * (0.5 + sensor / (1.0 + sensor))).astype(jnp.bfloat16)
    weight = visc.astype(jnp.float32)[None]
    flux_z = (weight * grad_z.astype(jnp.float32)).astype(jnp.bfloat16)
    flux_y = (weight * grad_y.astype(jnp.float32)).astype(jnp.bfloat16)
    div_z = lax.map(lambda field: zline_apply(field, dz_op), flux_z)
    div_y = lax.map(lambda field: yline_apply(field, dy_op), flux_y)
    total = state.astype(jnp.float32) + 0.5 * (div_y.astype(jnp.float32) + div_z.astype(jnp.float32))
    return total.astype(jnp.bfloat16)
```

```python
import jax
import jax.numpy as jnp
from jax import lax
from jax.sharding import PartitionSpec as P

F32 = jnp.float32
BF16 = jnp.bfloat16


def spread(block, axis):
    n = lax.axis_size(axis)
    copies = jnp.broadcast_to(block[None], (n, *block.shape))
    return lax.all_to_all(copies, axis, split_axis=0, concat_axis=0, tiled=True)


def rounded(left, right, dims):
    return lax.dot_general(left, right, (dims, ((), ())), preferred_element_type=F32).astype(BF16)


def on_device(state, visc_base, dz_op, dy_op):
    fields, planes, ylocal, zlocal = state.shape
    gz, gy = lax.axis_size("gz"), lax.axis_size("gy")
    ny, nz = dy_op.shape[0], dz_op.shape[0]
    parts = gz // planes
    lines = ylocal // parts
    cols = planes * zlocal

    st = jnp.transpose(state, (2, 0, 1, 3)).reshape(ylocal, fields * cols)
    vb = jnp.transpose(visc_base, (1, 0, 2)).reshape(ylocal, cols)
    whole = spread(st, "gy").reshape(ny, fields * cols)
    own = lax.dynamic_slice_in_dim(dy_op, lax.axis_index("gy") * ylocal, ylocal, 1)
    dens_y = rounded(own, whole[:, :cols], ((0,), (0,)))

    out = jnp.concatenate([st, dens_y, vb], axis=1)
    out = out.reshape(parts, lines, fields + 2, planes, zlocal)
    out = jnp.transpose(out, (3, 0, 2, 1, 4)).reshape(gz, (fields + 2) * lines * zlocal)
    got = lax.all_to_all(out, "gz", split_axis=0, concat_axis=0, tiled=True)
    got = got.reshape(gz, (fields + 2) * lines, zlocal)
    got = jnp.transpose(got, (1, 0, 2)).reshape((fields + 2) * lines, nz)
    grad_z = rounded(got[: fields * lines], dz_op, ((1,), (0,)))
    gz0 = grad_z[:lines].astype(F32)
    gy0 = got[fields * lines : (fields + 1) * lines].astype(F32)
    base = got[(fields + 1) * lines :].astype(F32)
    sensor = gy0**2 + gz0**2
    visc = (base * (0.5 + sensor / (1.0 + sensor))).astype(BF16)
    flux_z = (visc.astype(F32)[None] * grad_z.reshape(fields, lines, nz).astype(F32)).astype(BF16)
    div_z = rounded(flux_z.reshape(fields * lines, nz), dz_op, ((1,), (0,)))

    ret = jnp.concatenate([div_z, visc], axis=0).reshape((fields + 1) * lines, gz, zlocal)
    ret = jnp.transpose(ret, (1, 0, 2)).reshape(gz, (fields + 1) * lines * zlocal)
    ret = lax.all_to_all(ret, "gz", split_axis=0, concat_axis=0, tiled=True)
    ret = ret.reshape(planes, parts, fields + 1, lines, zlocal)
    ret = jnp.transpose(ret, (1, 3, 2, 0, 4)).reshape(ylocal, (fields + 1) * cols)

    grad_y = rounded(dy_op, whole, ((0,), (0,)))
    visc_all = spread(ret[:, fields * cols :], "gy").reshape(ny, cols)
    flux_y = (visc_all.astype(F32)[:, None] * grad_y.reshape(ny, fields, cols).astype(F32)).astype(BF16)
    div_y = rounded(own, flux_y.reshape(ny, fields * cols), ((0,), (0,)))
    total = st.astype(F32) + 0.5 * (div_y.astype(F32) + ret[:, : fields * cols].astype(F32))
    total = total.astype(BF16).reshape(ylocal, fields, planes, zlocal)
    return jnp.transpose(total, (1, 2, 0, 3))


def solution(mesh):
    return jax.shard_map(
        on_device,
        mesh=mesh,
        in_specs=(P(None, None, "gy", "gz"), P(None, "gy", "gz"), P(), P()),
        out_specs=P(None, None, "gy", "gz"),
        check_vma=False,
    )
```

```python
import jax
import jax.numpy as jnp
from jax import lax
from jax.sharding import PartitionSpec as P

F32 = jnp.float32
BF16 = jnp.bfloat16


def spread(block, axis):
    n = lax.axis_size(axis)
    copies = jnp.broadcast_to(block[None], (n, *block.shape))
    return lax.all_to_all(copies, axis, split_axis=0, concat_axis=0, tiled=True)


def rounded(left, right, dims):
    return lax.dot_general(left, right, (dims, ((), ())), preferred_element_type=F32).astype(BF16)


def gathered(block):
    gy = lax.axis_size("gy")
    held = block[None]
    for bit in (1, 2):
        other = lax.ppermute(held, "gy", [(i, i ^ bit) for i in range(gy)])
        held = jnp.concatenate([held, other], axis=0)
    parts = [held]
    for step in range(4, gy, 4):
        parts.append(lax.ppermute(held, "gy", [(i, (i + step) % gy) for i in range(gy)]))
    return jnp.concatenate(parts, axis=0)


def gathered_order():
    gy = lax.axis_size("gy")
    me = lax.axis_index("gy")
    return [lax.rem((me ^ (k & 3)) + gy - (k & ~3), gy) for k in range(gy)]


def section(state, visc_base, dz_op, dy_op):
    fields, planes, ylocal, zlocal = state.shape
    gz = lax.axis_size("gz")
    ny, nz = dy_op.shape[0], dz_op.shape[0]
    parts = gz // planes
    lines = ylocal // parts
    cols = planes * zlocal

    st = jnp.transpose(state, (2, 0, 1, 3)).reshape(ylocal, fields * cols)
    vb = jnp.transpose(visc_base, (1, 0, 2)).reshape(ylocal, cols)
    dens = spread(st[:, :cols], "gy").reshape(ny, cols)
    own = lax.dynamic_slice_in_dim(dy_op, lax.axis_index("gy") * ylocal, ylocal, 1)
    dens_y = rounded(own, dens, ((0,), (0,)))

    out = jnp.concatenate([st, dens_y, vb], axis=1)
    out = out.reshape(parts, lines, fields + 2, planes, zlocal)
    out = jnp.transpose(out, (3, 0, 2, 1, 4)).reshape(gz, (fields + 2) * lines * zlocal)
    got = lax.all_to_all(out, "gz", split_axis=0, concat_axis=0, tiled=True)
    rest = gathered(st[:, cols:]).reshape(ny, (fields - 1) * cols)
    rows = jnp.concatenate([lax.dynamic_slice_in_dim(dy_op, i * ylocal, ylocal, 0) for i in gathered_order()], axis=0)
    grad_r = rounded(rows, rest, ((0,), (0,)))
    grad_d = rounded(dy_op, dens, ((0,), (0,)))
    grad_y = lax.optimization_barrier(jnp.concatenate([grad_d, grad_r], axis=1))
    got = got.reshape(gz, (fields + 2) * lines, zlocal)
    got = lax.optimization_barrier(jnp.transpose(got, (1, 0, 2)).reshape((fields + 2) * lines, nz))
    grad_z = rounded(got[: fields * lines], dz_op, ((1,), (0,)))
    gz0 = grad_z[:lines].astype(F32)
    gy0 = got[fields * lines : (fields + 1) * lines].astype(F32)
    base = got[(fields + 1) * lines :].astype(F32)
    sensor = gy0**2 + gz0**2
    visc = (base * (0.5 + sensor / (1.0 + sensor))).astype(BF16)
    flux_z = (visc.astype(F32)[None] * grad_z.reshape(fields, lines, nz).astype(F32)).astype(BF16)
    div_z = rounded(flux_z.reshape(fields * lines, nz), dz_op, ((1,), (0,)))

    ret = jnp.concatenate([div_z, visc], axis=0).reshape((fields + 1) * lines, gz, zlocal)
    ret = jnp.transpose(ret, (1, 0, 2)).reshape(gz, (fields + 1) * lines * zlocal)
    ret = lax.all_to_all(ret, "gz", split_axis=0, concat_axis=0, tiled=True)
    ret = ret.reshape(planes, parts, fields + 1, lines, zlocal)
    ret = jnp.transpose(ret, (1, 3, 2, 0, 4)).reshape(ylocal, (fields + 1) * cols)

    visc_all = spread(ret[:, fields * cols :], "gy").reshape(ny, cols)
    flux_y = (visc_all.astype(F32)[:, None] * grad_y.reshape(ny, fields, cols).astype(F32)).astype(BF16)
    div_y = rounded(own, flux_y.reshape(ny, fields * cols), ((0,), (0,)))
    total = st.astype(F32) + 0.5 * (div_y.astype(F32) + ret[:, : fields * cols].astype(F32))
    total = total.astype(BF16).reshape(ylocal, fields, planes, zlocal)
    return jnp.transpose(total, (1, 2, 0, 3))


def solution(mesh):
    return jax.shard_map(
        section,
        mesh=mesh,
        in_specs=(P(None, None, "gy", "gz"), P(None, "gy", "gz"), P(), P()),
        out_specs=P(None, None, "gy", "gz"),
        check_vma=False,
    )
```
